768 devices in a mesh: gx: 16 (over y, x_hi), gy: 4 (over x_lo, core), gz: 12 (over z).
Axes of the slice: x: 4 (x_hi: 2, x_lo: 2; x = x_hi * 2 + x_lo), y: 8, z: 12, core: 2. Of those that a mesh axis runs over, the one named last changes fastest.
Arguments:
- flexibility: bfloat16 [16, 4, 12, 768, 768], P('gx', 'gy', 'gz'), may hold values from -6 to 6, as said below
- stiffness: bfloat16 [16, 4, 12, 768, 768], P('gx', 'gy', 'gz'), may hold values from -6 to 6, as said below
- local_load: float32 [16, 4, 12, 6, 128, 128], P('gx', 'gy', 'gz'), may hold values from -80 to 80
- face_map: int32 [16, 4, 12, 6, 128], P('gx', 'gy', 'gz'), may hold values from 0 to 127, each once within a row
- face_sign: int32 [16, 4, 12, 6, 128], P('gx', 'gy', 'gz'), may hold values from -1 to 1, as said below
Outputs:
- multipliers: float32 [16, 4, 12, 3, 128, 128], P('gx', 'gy', 'gz')
- residual: float32 [16, 4, 12, 3, 128, 128], P('gx', 'gy', 'gz')
The draws below stay inside these ranges and needn't reach their ends.
Inputs may be any that keep to these rules, and one draw needn't show every extreme that they name: `face_map`: each row is a permutation of 0 to 127. `face_sign`: every entry is +1 or -1, and the two subdomains sharing a face give each of its multipliers opposite signs. `flexibility`: each subdomain's matrix is symmetric positive definite. `stiffness`: each subdomain's matrix is symmetric positive definite.
All inputs are finite; a program needn't handle non-finite values.
Results may differ from the reference program's by a relative error of at most 0.011.
Values sent between devices are 32-bit elements; how exact they have to be, the bound alone decides.
No kernel may reach another device: no remote copies, remote signals or barrier semaphores. Data moves between devices by JAX's collectives and lax.ppermute only.
A program may use at most 32 MiB of HBM per device.

```python
import math
import jax
import jax.numpy as jnp
from jax import lax

FACE = 128
RESP = 128
ITERS = 2
SUB_X = 16
SUB_Y = 4
SUB_Z = 12


def operator_draw(key, scale_low, scale_high):
    order = 6 * FACE
    shape = (SUB_X, SUB_Y, SUB_Z, order, order)
    noise = jnp.clip(jax.random.normal(jax.random.fold_in(key, 1), shape, jnp.float32), -5.0, 5.0)
    coupling = (noise + jnp.swapaxes(noise, -1, -2)) * (0.42 / math.sqrt(2.0 * order))
    base = jnp.eye(order, dtype=jnp.float32) + coupling
    logs = jax.random.uniform(jax.random.fold_in(key, 2), shape[:-1], jnp.float32, math.log(scale_low), math.log(scale_high))
    roots = jnp.sqrt(jnp.exp(logs))
    return (roots[..., :, None] * base * roots[..., None, :]).astype(jnp.bfloat16)


def draw_flexibility(key, part):
    return operator_draw(jax.random.fold_in(key, 11), 0.5, 2.0)


def draw_stiffness(key, part):
    return operator_draw(jax.random.fold_in(key, 23), 0.5, 2.0)


def draw_face_sign(key, part):
    sign_bits = jax.random.randint(jax.random.fold_in(key, 5), (SUB_X, SUB_Y, SUB_Z, 3, FACE), 0, 2)
    lower_sign = 2 * sign_bits - 1
    stacked = []
    for dimension in range(3):
        lower_face = lower_sign[:, :, :, dimension]
        stacked.append(lower_face)
        stacked.append(-jnp.roll(lower_face, -1, axis=dimension))
    return jnp.stack(stacked, axis=3).astype(jnp.int32)


def draw_local_load(key, part):
    shape = (SUB_X, SUB_Y, SUB_Z, 6, FACE, RESP)
    pos_x = jnp.arange(SUB_X, dtype=jnp.float32) / max(SUB_X - 1, 1)
    pos_y = jnp.arange(SUB_Y, dtype=jnp.float32) / max(SUB_Y - 1, 1)
    pos_z = jnp.arange(SUB_Z, dtype=jnp.float32) / max(SUB_Z - 1, 1)
    rising = 3.0 ** ((pos_x[:, None, None] + pos_y[None, :, None] + pos_z[None, None, :]) / 3.0)
    column_scale = jnp.exp(jax.random.uniform(jax.random.fold_in(key, 3), (RESP,), jnp.float32, math.log(0.3), math.log(3.0)))
    base = jnp.clip(jax.random.normal(jax.random.fold_in(key, 4), shape, jnp.float32), -4.0, 4.0)
    amplitude = rising[:, :, :, None, None, None]
    return (base * amplitude * column_scale).astype(jnp.float32)


def setup_inputs(seed: int = 0) -> dict:
    keys = jax.random.split(jax.random.key(seed), 6)
    return {
        "flexibility": draw_flexibility(jax.random.fold_in(keys[5], 71), 0),
        "stiffness": draw_stiffness(jax.random.fold_in(keys[5], 71), 0),
        "local_load": draw_local_load(jax.random.fold_in(keys[5], 71), 0),
        "face_map": jax.vmap(lambda own: jax.random.permutation(own, FACE))(jax.random.split(keys[3], SUB_X * SUB_Y * SUB_Z * 6)).reshape((SUB_X, SUB_Y, SUB_Z, 6, FACE)).astype(jnp.int32),
        "face_sign": draw_face_sign(jax.random.fold_in(keys[5], 71), 0),
    }


def local_apply(operator, face_map, face_sign, vector):
    width = face_map.shape[-1]
    columns = vector.shape[-1]
    face_rows = (jnp.arange(6, dtype=jnp.int32)[:, None] * width + face_map).reshape(-1).astype(jnp.int32)
    signs = face_sign.astype(jnp.float32)[:, :, None]
    signed = (signs * vector).reshape(6 * width, columns)
    scattered = jnp.zeros((6 * width, columns), jnp.float32).at[face_rows].set(signed)
    product = jnp.dot(operator, scattered.astype(jnp.bfloat16), preferred_element_type=jnp.float32)
    gathered = product[face_rows].reshape(6, width, columns)
    return signs * gathered


def local_entry(packed):
    return local_apply(packed[0], packed[1], packed[2], packed[3])


def assemble(vector):
    assembled = []
    for dimension in range(3):
        lower_face = vector[:, :, :, 2 * dimension]
        upper_face = vector[:, :, :, 2 * dimension + 1]
        assembled.append(lower_face + jnp.roll(upper_face, 1, axis=dimension))
        assembled.append(upper_face + jnp.roll(lower_face, -1, axis=dimension))
    return jnp.stack(assembled, axis=3)


def apply_operator(operators, face_map, face_sign, vector):
    grid = vector.shape[:3]
    count = grid[0] * grid[1] * grid[2]
    order = operators.shape[-1]
    width = face_map.shape[-1]
    columns = vector.shape[-1]
    packed = (operators.reshape(count, order, order), face_map.reshape(count, 6, width),
              face_sign.reshape(count, 6, width), vector.reshape(count, 6, width, columns))
    locals_out = lax.map(local_entry, packed)
    return assemble(locals_out.reshape(vector.shape))


def inner(first, second):
    return jnp.sum(first[:, :, :, 0::2] * second[:, :, :, 0::2], axis=(0, 1, 2, 3, 4))


def reference(flexibility, stiffness, local_load, face_map, face_sign):
    residual = assemble(local_load)
    multipliers = jnp.zeros_like(residual)
    precond = apply_operator(stiffness, face_map, face_sign, residual)
    image_z = apply_operator(flexibility, face_map, face_sign, precond)
    gamma_now = inner(residual, precond)
    delta_now = inner(precond, image_z)
    step_size = gamma_now / delta_now
    direction = precond
    image_dir = image_z
    for iteration in range(ITERS):
        multipliers = multipliers + step_size * direction
        residual = residual - step_size * image_dir
        if iteration + 1 < ITERS:
            precond = apply_operator(stiffness, face_map, face_sign, residual)
            image_z = apply_operator(flexibility, face_map, face_sign, precond)
            gamma_new = inner(residual, precond)
            delta_now = inner(precond, image_z)
            conjugacy = gamma_new / gamma_now
            step_size = gamma_new / (delta_now - conjugacy * gamma_new / step_size)
            direction = precond + conjugacy * direction
            image_dir = image_z + conjugacy * image_dir
            gamma_now = gamma_new
    return multipliers[:, :, :, 0::2], residual[:, :, :, 0::2]
```

```python
import jax
import jax.numpy as jnp
from jax import lax
from jax.experimental import pallas as pl
from jax.experimental.pallas import tpu as pltpu
from jax.sharding import Mesh
from jax.sharding import PartitionSpec as P

GX = ("gx_0", "gx_1")
GY = ("gy_0", "gy_1")
GZ = ("gz",)
AXES = (GX, GY, GZ)
FACES = 6
VMEM_LIMIT = 16 * 2**20


def shift(array, axis, step):
    count = lax.axis_size(axis)
    pairs = [(i, (i + step) % count) for i in range(count)]
    return lax.ppermute(array, axis, pairs)


def exchange(faces):
    across = [None] * FACES
    for dim, axis in enumerate(AXES):
        across[2 * dim] = shift(faces[2 * dim + 1], axis, 1)
        across[2 * dim + 1] = shift(faces[2 * dim], axis, -1)
    return across


def exchange_up(faces):
    across = []
    for dim, axis in enumerate(AXES):
        across.append(shift(faces[2 * dim + 1], axis, 1))
    return across


def vmem_spec():
    return pl.BlockSpec(memory_space=pltpu.VMEM)


def on_chip(arrays):
    return [pltpu.with_memory_space_constraint(array, pltpu.VMEM) for array in arrays]


def reorder_body(operator_ref, map_ref, sign_ref, out_ref, half_ref):
    width = map_ref.shape[1]
    rows = lax.broadcasted_iota(jnp.int32, (width, width), 0)
    select = []
    for face in range(FACES):
        hit = rows == map_ref[face : face + 1, :]
        signs = sign_ref[face : face + 1, :].astype(jnp.float32)
        select.append(jnp.where(hit, jnp.broadcast_to(signs, (width, width)), 0.0))
    for face in range(FACES):
        span = slice(face * width, (face + 1) * width)
        half_ref[:, span] = jnp.dot(
            operator_ref[:, span],
            select[face].astype(jnp.bfloat16),
            preferred_element_type=jnp.float32,
        ).astype(jnp.bfloat16)
    for face in range(FACES):
        span = slice(face * width, (face + 1) * width)
        out_ref[span, :] = jnp.dot(
            select[face].T.astype(jnp.bfloat16),
            half_ref[span, :],
            preferred_element_type=jnp.float32,
        ).astype(jnp.bfloat16)


def reorder(operator, maps, signs):
    order = operator.shape[0]
    return pl.pallas_call(
        reorder_body,
        out_shape=pltpu.VMEM((order, order), jnp.bfloat16),
        in_specs=[vmem_spec()] * 3,
        out_specs=vmem_spec(),
        scratch_shapes=[pltpu.VMEM((order, order), jnp.bfloat16)],
        compiler_params=pltpu.CompilerParams(vmem_limit_bytes=VMEM_LIMIT),
        name="reorder",
    )(operator, maps, signs)


def product_body(*refs):
    operator_ref = refs[0]
    own = refs[1 : 1 + FACES]
    across = refs[1 + FACES : 1 + 2 * FACES]
    outs = refs[1 + 2 * FACES :]
    local = outs[:FACES]
    dot_ref = outs[FACES]
    kept = outs[FACES + 1]
    width = own[0].shape[0]
    full = [own[face][...] + across[face][...] for face in range(FACES)]
    for dim in range(3):
        kept[dim] = full[2 * dim]
    full = jnp.concatenate(full, axis=0)
    high = full.astype(jnp.bfloat16)
    low = (full - high.astype(jnp.float32)).astype(jnp.bfloat16)
    both = jnp.concatenate([high, low], axis=1)
    result = jnp.dot(operator_ref[...], both, preferred_element_type=jnp.float32)
    columns = full.shape[1]
    result = result[:, :columns] + result[:, columns:]
    for face in range(FACES):
        local[face][...] = result[face * width : (face + 1) * width, :]
    dot_ref[...] = jnp.sum(full * result, axis=0, keepdims=True)


def product(operator, own, across):
    width, columns = own[0].shape
    face = pltpu.VMEM((width, columns), jnp.float32)
    outs = pl.pallas_call(
        product_body,
        out_shape=[face] * FACES
        + [
            pltpu.VMEM((1, columns), jnp.float32),
            pltpu.VMEM((3, width, columns), jnp.float32),
        ],
        in_specs=[vmem_spec()] * (1 + 2 * FACES),
        out_specs=[vmem_spec()] * (FACES + 2),
        compiler_params=pltpu.CompilerParams(vmem_limit_bytes=VMEM_LIMIT),
        name="product",
    )(*on_chip([operator, *own, *across]))
    return outs[:FACES], outs[FACES], outs[FACES + 1]


def finish_body(sums_ref, r0_ref, z0_ref, w0_ref, u_ref, v0, v2, v4, a0, a2, a4, mult_ref, res_ref):
    gamma = sums_ref[0:1, :]
    delta = sums_ref[1:2, :]
    eps = sums_ref[2:3, :]
    zeta = sums_ref[3:4, :]
    step = gamma / delta
    gamma_new = step * (step * eps) - gamma
    delta_new = delta - 2.0 * (step * eps) + step * (step * zeta)
    beta = gamma_new / gamma
    step_new = gamma_new / (delta_new - beta * gamma_new / step)
    first = step + step_new * (1.0 + beta)
    second = step_new * step
    for dim, (own, across) in enumerate(((v0, a0), (v2, a2), (v4, a4))):
        mult_ref[dim] = first * z0_ref[dim] - second * u_ref[dim]
        image = own[...] + across[...]
        res_ref[dim] = r0_ref[dim] - first * w0_ref[dim] + second * image


def finish(sums, r0, z0, w0, u, own, across):
    shape = jax.ShapeDtypeStruct(r0.shape, jnp.float32)
    return pl.pallas_call(
        finish_body,
        out_shape=[shape, shape],
        in_specs=[vmem_spec()] * 11,
        out_specs=[vmem_spec()] * 2,
        compiler_params=pltpu.CompilerParams(vmem_limit_bytes=VMEM_LIMIT),
        name="finish",
    )(*on_chip([sums, r0, z0, w0, u, own[0], own[2], own[4], *across]))


def total(parts):
    for group in (GY + GZ, GX):
        count = lax.axis_size(group)
        spread = jnp.broadcast_to(parts[None], (count,) + parts.shape)
        parts = jnp.sum(lax.all_to_all(spread, group, 0, 0), axis=0)
    return parts


def shards(flexibility, stiffness, local_load, face_map, face_sign):
    maps = face_map[0, 0, 0]
    signs = face_sign[0, 0, 0]
    load = local_load[0, 0, 0]
    own = [load[face] for face in range(FACES)]
    across = exchange(own)
    stiff = reorder(stiffness[0, 0, 0], maps, signs)
    flex = reorder(flexibility[0, 0, 0], maps, signs)
    own, gamma, r0 = product(stiff, own, across)
    own, delta, z0 = product(flex, own, exchange(own))
    own, eps, w0 = product(stiff, own, exchange(own))
    own, zeta, u = product(flex, own, exchange(own))
    across = exchange_up(own)
    sums = total(jnp.concatenate([gamma, delta, eps, zeta], axis=0))
    mult, res = finish(sums, r0, z0, w0, u, own, across)
    return mult[None, None, None], res[None, None, None]


def solution(mesh):
    split = Mesh(
        mesh.devices.reshape(mesh.shape["gx"] // 2, 2, mesh.shape["gy"] // 2, 2, mesh.shape["gz"]),
        ("gx_0", "gx_1", "gy_0", "gy_1", "gz"),
    )
    vector = P(GX, GY, "gz", None, None, None)
    matrix = P(GX, GY, "gz", None, None)
    return jax.shard_map(
        shards,
        mesh=split,
        in_specs=(matrix, matrix, vector, matrix, matrix),
        out_specs=(vector, vector),
        check_vma=False,
    )
```
